1024 devices in a mesh: ex: 64 (over z, y_hi), ez: 16 (over y_lo, x, core).
Axes of the slice: x: 4, y: 8 (y_hi: 4, y_lo: 2; y = y_hi * 2 + y_lo), z: 16, core: 2. Of those that a mesh axis runs over, the one named last changes fastest.
Arguments:
- potential: float32 [512, 16, 128], P('ex', None, 'ez'), may hold values from -1.5 to 0.5
- basis_start: bfloat16 [64, 16, 2, 1728, 128], P('ex', 'ez'), may hold values from -6 to 6
Outputs:
- diagonal_blocks: float32 [64, 128, 16, 2, 128], P('ex', 'ez')
- coupling_blocks: float32 [64, 128, 16, 2, 3, 128], P('ex', 'ez')
The draws below stay inside these ranges and needn't reach their ends.
All inputs are finite; a program needn't handle non-finite values.
Results may differ from the reference program's by a relative error of at most 0.0003.
Values sent between devices are 32-bit elements; how exact they have to be, the bound alone decides.
A program may use at most 32 MiB of HBM per device.

```python
import jax
import jax.numpy as jnp
from jax import lax

G = 8
NB = 128
EY = 2
FILTER = 3
NXE = 64
NZE = 16
EXT = 12
EXT3 = 1728
NXG = 512
NYG = 16
NZG = 128


def shard_levels(own_key, extent, pieces, least, high):
    factor_of, own = 1.0, jax.random.fold_in(own_key, 6)
    for dim, shards_of in pieces:
        draws = jnp.exp(jax.random.uniform(jax.random.fold_in(own, dim), (shards_of,), jnp.float32, least / len(pieces), high / len(pieces)))
        factor_of = factor_of * jnp.repeat(draws, extent[dim] // shards_of).reshape([-1 if axis == dim else 1 for axis in range(len(extent))])
    return factor_of


def normal_values(key, dims, spread, limit, split=(), held_as=jnp.bfloat16):
    drawn = jax.random.normal(key, dims, jnp.float32) * spread
    if len(split) > 0:
        drawn = shard_levels(key, dims, split, -0.22, 0.18) * drawn
    return jnp.clip(drawn, min=-limit, max=limit).astype(held_as)


def setup_inputs(seed: int = 0) -> dict:
    keys = jax.random.split(jax.random.key(seed), 3)
    potential = jnp.clip(-1.5 + 2.0 * jax.random.uniform(keys[0], (NXG, NYG, NZG), jnp.float32) ** shard_levels(keys[0], (NXG, NYG, NZG), ((0, 64), (2, 16)), -0.2, 0.2), -1.5, 0.5)
    basis_start = normal_values(keys[1], (NXE, NZE, EY, EXT3, NB), 1.0, 6.0, ((0, 64), (1, 16)))
    return dict(potential=potential, basis_start=basis_start)


center = 6.5
halfwidth = 5.5
penalty = 1.0
highest = lax.Precision.HIGHEST

def apply_hamiltonian(field, potential_box):
    padded = jnp.pad(field, ((1, 1), (1, 1), (1, 1), (0, 0)))
    beside = padded[2:, 1:-1, 1:-1] + padded[:-2, 1:-1, 1:-1]
    beside = beside + padded[1:-1, 2:, 1:-1] + padded[1:-1, :-2, 1:-1]
    beside = beside + padded[1:-1, 1:-1, 2:] + padded[1:-1, 1:-1, :-2]
    return 3.0 * field - 0.5 * beside + potential_box[:, :, :, None] * field

def local_basis(initial, potential_box):
    box_side = potential_box.shape[0]
    margin = (box_side - G) // 2
    columns = initial.shape[-1]
    previous = initial.astype(jnp.float32).reshape(box_side, box_side, box_side, columns)
    current = (apply_hamiltonian(previous, potential_box) - center * previous) / halfwidth
    for iteration in range(FILTER - 1):
        following = 2.0 / halfwidth * (apply_hamiltonian(current, potential_box) - center * current) - previous
        previous, current = (current, following)
    flattened = current.reshape(box_side ** 3, columns)
    intersection = lax.dot_general(flattened.astype(jnp.float32), flattened.astype(jnp.float32), (((0,), (0,)), ((), ())), precision=highest, preferred_element_type=jnp.float32)
    factor = jnp.linalg.cholesky(intersection)
    interior = current[margin:margin + G, margin:margin + G, margin:margin + G].reshape(G ** 3, columns)
    solved = jax.scipy.linalg.solve_triangular(factor, interior.T, lower=True)
    return solved.T.reshape(G, G, G, columns)

def forward_difference(basis, dimension):
    differences = jnp.diff(basis, axis=dimension)
    widths = [(0, 0)] * basis.ndim
    widths[dimension] = (0, 1)
    return jnp.pad(differences, widths)

def volume_terms(basis, inner_potential):
    gradients = [forward_difference(basis, dimension) for dimension in (1, 2, 3)]
    weighted = jnp.concatenate([0.5 * gradients[0], 0.5 * gradients[1], 0.5 * gradients[2], inner_potential[..., None] * basis], axis=1)
    plain_side = jnp.concatenate(gradients + [basis], axis=1)
    elements = basis.shape[0]
    columns = basis.shape[-1]
    weighted = weighted.reshape(elements, -1, columns)
    plain_side = plain_side.reshape(elements, -1, columns)
    return jnp.einsum('epi,epj->iej', weighted, plain_side, precision=highest)

def face_traces(basis):
    points = basis.shape[1]
    elements = basis.shape[0]
    columns = basis.shape[-1]
    plus_layers = []
    minus_layers = []
    for dimension in (1, 2, 3):
        outer_last = lax.index_in_dim(basis, points - 1, dimension, keepdims=False)
        inner_last = lax.index_in_dim(basis, points - 2, dimension, keepdims=False)
        outer_first = lax.index_in_dim(basis, 0, dimension, keepdims=False)
        inner_first = lax.index_in_dim(basis, 1, dimension, keepdims=False)
        plus_layers.append(jnp.stack([outer_last, outer_last - inner_last], axis=1))
        minus_layers.append(jnp.stack([outer_first, inner_first - outer_first], axis=1))
    plus_traces = jnp.stack(plus_layers, axis=1).reshape(elements, 3, 2, points * points, columns)
    minus_traces = jnp.stack(minus_layers, axis=1).reshape(elements, 3, 2, points * points, columns)
    return (plus_traces, minus_traces)

def face_diagonal(plus_traces, minus_traces):
    side_plus = -0.25 * plus_traces[:, :, 1] + 0.5 * penalty * plus_traces[:, :, 0]
    side_minus = 0.25 * minus_traces[:, :, 1] + 0.5 * penalty * minus_traces[:, :, 0]
    direct = jnp.einsum('ekpi,ekpj->iej', side_plus, plus_traces[:, :, 0], precision=highest)
    direct = direct + jnp.einsum('ekpi,ekpj->iej', side_minus, minus_traces[:, :, 0], precision=highest)
    mirror = jnp.einsum('ekpi,ekpj->iej', plus_traces[:, :, 0], side_plus, precision=highest)
    mirror = mirror + jnp.einsum('ekpi,ekpj->iej', minus_traces[:, :, 0], side_minus, precision=highest)
    return direct + mirror

def coupling(plus_traces, next_traces):
    weighted = 0.25 * plus_traces[:, :, 1] - penalty * plus_traces[:, :, 0]
    result = jnp.einsum('ekpi,ekpj->iekj', weighted, next_traces[:, :, 0], precision=highest)
    return result - 0.25 * jnp.einsum('ekpi,ekpj->iekj', plus_traces[:, :, 0], next_traces[:, :, 1], precision=highest)

def reference(potential, basis_start):
    margin = G // 4
    padded = jnp.pad(potential, margin, mode='wrap')

    def slab_basis(x_index):
        slab_start = lax.dynamic_index_in_dim(basis_start, x_index, 0, keepdims=False).reshape(NZE * EY, EXT3, NB)

        def one_element(element):
            z_index = element // EY
            y_index = element % EY
            potential_box = lax.dynamic_slice(padded, (x_index * G, y_index * G, z_index * G), (EXT, EXT, EXT))
            initial = lax.dynamic_index_in_dim(slab_start, element, 0, keepdims=False)
            return local_basis(initial, potential_box)
        return lax.map(one_element, jnp.arange(NZE * EY, dtype=jnp.int32))

    def slab_potential(x_index):
        layers = lax.dynamic_slice_in_dim(potential, x_index * G, G, 0)
        return layers.reshape(G, EY, G, NZE, G).transpose(3, 1, 0, 2, 4).reshape(NZE * EY, G, G, G)

    def assemble(carry, x_index):
        basis = slab_basis(x_index)
        plus_traces, minus_traces = face_traces(basis)
        diagonal = volume_terms(basis, slab_potential(x_index)) + face_diagonal(plus_traces, minus_traces)
        own_minus = minus_traces.reshape(NZE, EY, 3, 2, G * G, NB)
        from_y = jnp.roll(own_minus[:, :, 1], -1, axis=1).reshape(NZE * EY, 2, G * G, NB)
        from_z = jnp.roll(own_minus[:, :, 2], -1, axis=0).reshape(NZE * EY, 2, G * G, NB)
        next_traces = jnp.stack([carry, from_y, from_z], axis=1)
        coupled = coupling(plus_traces, next_traces)
        return (minus_traces[:, 0], (diagonal.reshape(NB, NZE, EY, NB), coupled.reshape(NB, NZE, EY, 3, NB)))
    first_minus = face_traces(slab_basis(jnp.int32(0)))[1][:, 0]
    unused, outputs = lax.scan(assemble, first_minus, jnp.arange(NXE, dtype=jnp.int32), reverse=True)
    return (outputs[0], outputs[1])
```

```python
import jax
import jax.numpy as jnp
from jax import lax
from jax.experimental import pallas as pl
from jax.experimental.pallas import tpu as pltpu
from jax.sharding import PartitionSpec as P

G, BOX, NB, EY = 8, 12, 128, 2
ROWS = BOX ** 3
SLAB = BOX * BOX
BLOCKS = NB // 8
HIGHEST = lax.Precision.HIGHEST
F32 = jnp.float32
BF16 = jnp.bfloat16
MESH = pl.DeviceIdType.MESH


def dot(a, b, dims):
    return lax.dot_general(a, b, (dims, ((), ())), precision=HIGHEST, preferred_element_type=F32)


def sub_row(tile, row):
    return jnp.broadcast_to(tile[row:row + 1, :], (8, NB))


def lane_col(tile, lane):
    return jnp.broadcast_to(tile[:, lane:lane + 1], (8, NB))


def factor_inverse(tiles_of, inv_ref):
    sub = lax.broadcasted_iota(jnp.int32, (8, NB), 0)
    lane = lax.broadcasted_iota(jnp.int32, (8, NB), 1)
    tiles = [list(t) for t in tiles_of]
    for k in range(BLOCKS):
        inside = (lane >= 8 * k) & (lane < 8 * k + 8)
        for e in range(len(tiles)):
            T = tiles[e]
            C = [lane_col(T[k], 8 * k + m) for m in range(8)]
            J = jnp.where(inside, jnp.where(lane - 8 * k == sub, 1.0, 0.0).astype(F32), T[k])
            forward = J
            rdiag = jnp.zeros((8, NB), F32)
            for j in range(8):
                r = 1.0 / sub_row(C[j], j)
                mult = jnp.where(sub == j, 0.0, C[j] * r)
                row = sub_row(J, j)
                forward = jnp.where(sub == j, J, forward)
                rdiag = jnp.where(sub == j, r, rdiag)
                for m in range(j + 1, 8):
                    C[m] = C[m] - mult * sub_row(C[m], j)
                J = J - mult * row
            J = J * rdiag
            inv_ref[e, 8 * k:8 * k + 8, :] = jnp.where(lane <= sub + 8 * k, forward * jnp.sqrt(rdiag), 0.0)
            if k + 1 < BLOCKS:
                rows = [sub_row(J, m) for m in range(8)]
                for t in range(k + 1, BLOCKS):
                    old = T[t]
                    new = jnp.where(inside, 0.0, old)
                    for m in range(8):
                        new = new - lane_col(old, 8 * k + m) * rows[m]
                    T[t] = new


def local_kernel(pot_ref, basis_ref, first_ref, left_ref, right_ref,
                 scaled, fa, fb, inner, stencil, gram, inv, traces):
    sub = lax.broadcasted_iota(jnp.int32, (8, NB), 0)
    zero_slab = jnp.zeros((SLAB, NB), F32)
    for buf in (fa, fb):
        for e in range(EY):
            buf[e, 0:SLAB, :] = zero_slab
            buf[e, SLAB + ROWS:2 * SLAB + ROWS, :] = zero_slab

    @pl.loop(0, BOX)
    def _(x):
        low = (pot_ref[x, 0:8, :] - 3.5) * (1.0 / 5.5)
        high = (pot_ref[x, 8:16, :] - 3.5) * (1.0 / 5.5)
        for y in range(16):
            a = lane_col(low, y)
            b = lane_col(high, y)
            for e in range(EY):
                at = (y - 8 * e + 2) % 16
                if at < BOX:
                    base = x * SLAB + at * BOX
                    scaled[e, pl.ds(base, 8), :] = a
                    scaled[e, pl.ds(base + 8, 4), :] = b[0:4, :]

    @pl.loop(0, BOX)
    def _(x):
        for e in range(EY):
            base = pl.multiple_of(x * SLAB, 16)
            fa[e, pl.ds(pl.multiple_of(base + SLAB, 8), SLAB), :] = basis_ref[e, pl.ds(base, SLAB), :].astype(F32)

    def sweep(src, dst, older):
        @pl.loop(0, BOX)
        def _(x):
            for e in range(EY):
                for t in range(SLAB // 8):
                    at = pl.multiple_of(x * SLAB + 8 * t, 8)
                    o = SLAB + at
                    center = src[e, pl.ds(o, 8), :]
                    beside = src[e, pl.ds(o - SLAB, 8), :] + src[e, pl.ds(o + SLAB, 8), :]
                    if t > 0:
                        v = src[e, pl.ds(o - BOX, 8), :]
                        beside = beside + (jnp.where(sub < 4, 0.0, v) if t == 1 else v)
                    if t < SLAB // 8 - 1:
                        v = src[e, pl.ds(o + BOX, 8), :]
                        beside = beside + (jnp.where(sub >= 4, 0.0, v) if t == SLAB // 8 - 2 else v)
                    v = src[e, pl.ds(o - 1, 8), :]
                    beside = beside + (v if t % 3 == 2 else jnp.where(sub == (0, 4)[t % 3], 0.0, v))
                    v = src[e, pl.ds(o + 1, 8), :]
                    beside = beside + (v if t % 3 == 0 else jnp.where(sub == (0, 3, 7)[t % 3], 0.0, v))
                    a = scaled[e, pl.ds(at, 8), :]
                    if older is None:
                        new = a * center - (0.5 / 5.5) * beside
                    else:
                        new = 2.0 * (a * center) - (1.0 / 5.5) * beside - older[e, pl.ds(o, 8), :]
                    dst[e, pl.ds(o, 8), :] = new

    sweep(fa, fb, None)
    sweep(fb, fa, fa)
    sweep(fa, fb, fb)

    for e in range(EY):
        full = fb[e, SLAB:SLAB + ROWS, :]
        high = full.astype(BF16)
        rest = (full - high.astype(F32)).astype(BF16)
        both = jnp.concatenate([high, rest], axis=1)
        prod = lax.dot_general(both, both, (((0,), (0,)), ((), ())), preferred_element_type=F32)
        cross = prod[0:NB, NB:2 * NB]
        gram[e] = prod[0:NB, 0:NB] + (cross + cross.T) + prod[NB:2 * NB, NB:2 * NB]

    factor_inverse([[gram[e, 8 * t:8 * t + 8, :] for t in range(BLOCKS)] for e in range(EY)], inv)

    up = jnp.where(sub == 0, 0.0, jnp.where((sub == 1) | (sub == 7), 0.25, 0.5))
    down = jnp.where(sub == 7, 0.0, jnp.where((sub == 0) | (sub == 6), 0.25, 0.5))

    def edge(i):
        return 0.25 if i in (0, 6) else 0.5

    for e in range(EY):
        for x in range(G):
            for y in range(G):
                p = (x + 2) * SLAB + (y + 2) * BOX + 2
                inner[e, 64 * x + 8 * y:64 * x + 8 * y + 8, :] = fb[e, SLAB + p:SLAB + p + 8, :]
    for e in range(EY):
        def tile(x, y):
            return inner[e, 64 * x + 8 * y:64 * x + 8 * y + 8, :]
        for x in range(G):
            for y in range(G):
                p = (x + 2) * SLAB + (y + 2) * BOX + 2
                c = tile(x, y)
                out = (5.5 * scaled[e, p:p + 8, :] + 6.5) * c
                if x > 0:
                    out = out - edge(x - 1) * tile(x - 1, y)
                if x < G - 1:
                    out = out - edge(x) * tile(x + 1, y)
                if y > 0:
                    out = out - edge(y - 1) * tile(x, y - 1)
                if y < G - 1:
                    out = out - edge(y) * tile(x, y + 1)
                out = out - up * pltpu.roll(c, 1, 0) - down * pltpu.roll(c, 7, 0)
                stencil[64 * x + 8 * y:64 * x + 8 * y + 8, :] = out
        raw = dot(inner[e], stencil[...], ((0,), (0,)))
        linv = inv[e]
        half = dot(linv, raw, ((1,), (0,)))
        diag = dot(half, linv, ((1,), (1,)))
        for r in range(BLOCKS):
            first_ref[r, e] = diag[8 * r:8 * r + 8, :]

        def layer(d, i):
            if d == 0:
                return inner[e, 64 * i:64 * i + 64, :]
            if d == 1:
                return jnp.concatenate([tile(x, i) for x in range(G)], axis=0)
            return inner[e, pl.ds(i, 64, stride=8), :]
        rows = []
        for d in range(3):
            last = layer(d, 7)
            rows += [-0.5 * last - 0.25 * layer(d, 6), -0.25 * last, layer(d, 0), layer(d, 1)]
        traces[e] = dot(jnp.concatenate(rows, axis=0), linv, ((1,), (1,)))
        for s, d in enumerate((0, 2)):
            left_ref[s, e] = traces[e, 256 * d:256 * d + 128, :]
            right_ref[s, e] = traces[e, 256 * d + 128:256 * d + 256, :]
    for e in range(EY):
        cy = dot(traces[e, 256:384, :], traces[1 - e, 384:512, :], ((0,), (0,)))
        for r in range(BLOCKS):
            first_ref[r, EY + e] = cy[8 * r:8 * r + 8, :]


def local_call(pot, basis):
    vm = pl.BlockSpec(memory_space=pltpu.VMEM)
    return pl.pallas_call(
        local_kernel,
        out_shape=(
            jax.ShapeDtypeStruct((BLOCKS, 2 * EY, 8, NB), F32),
            jax.ShapeDtypeStruct((2, EY, NB, NB), F32),
            jax.ShapeDtypeStruct((2, EY, NB, NB), F32),
        ),
        in_specs=[vm, vm],
        out_specs=(vm, vm, vm),
        scratch_shapes=[
            pltpu.VMEM((EY, ROWS, NB), F32),
            pltpu.VMEM((EY, ROWS + 2 * SLAB, NB), F32),
            pltpu.VMEM((EY, ROWS + 2 * SLAB, NB), F32),
            pltpu.VMEM((EY, G ** 3, NB), F32),
            pltpu.VMEM((G ** 3, NB), F32),
            pltpu.VMEM((EY, NB, NB), F32),
            pltpu.VMEM((EY, NB, NB), F32),
            pltpu.VMEM((EY, 768, NB), F32),
        ],
        compiler_params=pltpu.CompilerParams(vmem_limit_bytes=40 * 2**20),
    )(pot, basis)


def halo_kernel(block_ref, out_ref, low_x, high_x, low_z, high_z, corner, send_sem, recv_sem):
    ex, ez = lax.axis_index("ex"), lax.axis_index("ez")
    nx, nz = lax.axis_size("ex"), lax.axis_size("ez")
    xs = {-1: lax.rem(ex + nx - 1, nx), 0: ex, 1: lax.rem(ex + 1, nx)}
    zs = {-1: lax.rem(ez + nz - 1, nz), 0: ez, 1: lax.rem(ez + 1, nz)}
    steps = [(1, 0), (-1, 0), (0, 1), (0, -1), (1, 1), (1, -1), (-1, 1), (-1, -1)]
    barrier = pltpu.get_barrier_semaphore()
    for dx, dz in steps:
        pl.semaphore_signal(barrier, inc=1, device_id=(xs[dx], zs[dz]), device_id_type=MESH)
    pl.semaphore_wait(barrier, len(steps))
    landing = [low_x, high_x, low_z, high_z, corner.at[0], corner.at[1], corner.at[2], corner.at[3]]
    copies = []
    for n, (dx, dz) in enumerate(steps):
        if dx == 1:
            part = block_ref.at[pl.ds(G - 2, 2)]
        elif dx == -1:
            part = block_ref.at[pl.ds(0, 2)]
        else:
            part = block_ref
        copies.append(pltpu.make_async_remote_copy(
            src_ref=part, dst_ref=landing[n], send_sem=send_sem.at[n], recv_sem=recv_sem.at[n],
            device_id=(xs[dx], zs[dz]), device_id_type=MESH))
    for copy in copies:
        copy.start()
    for copy in copies:
        copy.wait()
    for x in range(BOX):
        if x < 2:
            low, mid, high = corner[0, x], low_x[x], corner[1, x]
        elif x < 2 + G:
            low, mid, high = low_z[x - 2], block_ref[x - 2], high_z[x - 2]
        else:
            low, mid, high = corner[2, x - 2 - G], high_x[x - 2 - G], corner[3, x - 2 - G]
        out_ref[x, 0:8, :] = jnp.concatenate([low[6:8], mid[0:6]], axis=0)
        out_ref[x, 8:16, :] = jnp.concatenate([mid[6:8], high[0:6]], axis=0)


def halo_call(block):
    vm = pl.BlockSpec(memory_space=pltpu.VMEM)
    part = (G, 2 * G)
    return pl.pallas_call(
        halo_kernel,
        out_shape=jax.ShapeDtypeStruct((BOX, 16, 2 * G), F32),
        in_specs=[vm],
        out_specs=vm,
        scratch_shapes=[
            pltpu.VMEM((2,) + part, F32),
            pltpu.VMEM((2,) + part, F32),
            pltpu.VMEM((G,) + part, F32),
            pltpu.VMEM((G,) + part, F32),
            pltpu.VMEM((4, 2) + part, F32),
            pltpu.SemaphoreType.DMA((8,)),
            pltpu.SemaphoreType.DMA((8,)),
        ],
        compiler_params=pltpu.CompilerParams(collective_id=0, has_side_effects=True),
    )(block)


def exchange_kernel(first_ref, left_ref, right_ref, diag_ref, coup_ref,
                    got_first, got_right, second, got_second,
                    right_send, right_recv, send_sem, recv_sem, own_sem):
    ex, ez = lax.axis_index("ex"), lax.axis_index("ez")
    nx, nz = lax.axis_size("ex"), lax.axis_size("ez")
    below, above = lax.rem(ex + nx - 1, nx), lax.rem(ex + 1, nx)
    peers = [lax.rem(ez + k, nz) for k in range(1, nz)]
    barrier = pltpu.get_barrier_semaphore()
    for target in [(below, ez), (above, ez)] + [(ex, p) for p in peers]:
        pl.semaphore_signal(barrier, inc=1, device_id=target, device_id_type=MESH)
    pl.semaphore_wait(barrier, nz + 1)

    traces = []
    for s, target in enumerate([(below, ez), (ex, peers[-1])]):
        traces.append(pltpu.make_async_remote_copy(
            src_ref=right_ref.at[s], dst_ref=got_right.at[s],
            send_sem=right_send.at[s], recv_sem=right_recv.at[s],
            device_id=target, device_id_type=MESH))
        traces[s].start()

    def spread(half, source, landing):
        copies = []
        for k, peer in enumerate(peers):
            copies.append(pltpu.make_async_remote_copy(
                src_ref=source.at[peer], dst_ref=landing.at[ez],
                send_sem=send_sem.at[half, k], recv_sem=recv_sem.at[half, k],
                device_id=(ex, peer), device_id_type=MESH))
            copies[k].start()
        own = pltpu.make_async_copy(source.at[ez], landing.at[ez], own_sem.at[half])
        own.start()
        return copies, own

    first_copies, first_own = spread(0, first_ref, got_first)
    for s in range(2):
        traces[s].wait_recv()
        for e in range(EY):
            block = dot(left_ref[s, e], got_right[s, e], ((0,), (0,)))
            for r in range(BLOCKS):
                second[r, s * EY + e] = block[8 * r:8 * r + 8, :]
    second_copies, second_own = spread(1, second, got_second)

    for copy in first_copies:
        copy.wait_recv()
    first_own.wait()

    @pl.loop(0, BLOCKS)
    def _(z):
        for e in range(EY):
            diag_ref[pl.ds(z * EY + e, 8, stride=BLOCKS * EY), :] = got_first[z, e]
            coup_ref[pl.ds(z * 3 * EY + EY + e, 8, stride=BLOCKS * 3 * EY), :] = got_first[z, EY + e]

    for copy in second_copies:
        copy.wait_recv()
    second_own.wait()

    @pl.loop(0, BLOCKS)
    def _(z):
        for e in range(EY):
            for s in range(2):
                coup_ref[pl.ds(z * 3 * EY + 2 * s * EY + e, 8, stride=BLOCKS * 3 * EY), :] = got_second[z, s * EY + e]

    for copy in traces + first_copies + second_copies:
        copy.wait_send()


def exchange_call(first, left, right):
    vm = pl.BlockSpec(memory_space=pltpu.VMEM)
    part = (BLOCKS, 2 * EY, 8, NB)
    return pl.pallas_call(
        exchange_kernel,
        out_shape=(
            jax.ShapeDtypeStruct((8 * BLOCKS * EY, NB), F32),
            jax.ShapeDtypeStruct((8 * BLOCKS * 3 * EY, NB), F32),
        ),
        in_specs=[vm] * 3,
        out_specs=(vm, vm),
        scratch_shapes=[
            pltpu.VMEM(part, F32),
            pltpu.VMEM((2, EY, NB, NB), F32),
            pltpu.VMEM(part, F32),
            pltpu.VMEM(part, F32),
            pltpu.SemaphoreType.DMA((2,)),
            pltpu.SemaphoreType.DMA((2,)),
            pltpu.SemaphoreType.DMA((2, BLOCKS - 1)),
            pltpu.SemaphoreType.DMA((2, BLOCKS - 1)),
            pltpu.SemaphoreType.DMA((2,)),
        ],
        compiler_params=pltpu.CompilerParams(collective_id=1, has_side_effects=True),
    )(first, left, right)


def local(potential, basis_start):
    halo = halo_call(jnp.transpose(potential, (0, 2, 1)))
    first, left, right = local_call(halo, basis_start.reshape(EY, ROWS, NB))
    diag, coup = exchange_call(first, left, right)
    coup = coup.reshape(8, BLOCKS, 3, EY, NB).transpose(0, 1, 3, 2, 4)
    return diag.reshape(1, 8, BLOCKS, EY, NB), coup[None]


def solution(mesh):
    return jax.shard_map(
        local,
        mesh=mesh,
        in_specs=(P("ex", None, "ez"), P("ex", "ez", None, None, None)),
        out_specs=(P("ex", "ez", None, None, None), P("ex", "ez", None, None, None, None)),
        check_vma=False,
    )
```

```python
import jax
import jax.numpy as jnp
from jax import lax
from jax.experimental import pallas as pl
from jax.experimental.pallas import tpu as pltpu
from jax.sharding import PartitionSpec as P

G, BOX, NB, EY = 8, 12, 128, 2
ROWS = BOX ** 3
SLAB = BOX * BOX
BLOCKS = NB // 8
HIGHEST = lax.Precision.HIGHEST
F32 = jnp.float32
BF16 = jnp.bfloat16
MESH = pl.DeviceIdType.MESH
SIDES = ((1, 0), (-1, 0), (0, 1), (0, -1), (1, 1), (1, -1), (-1, 1), (-1, -1))
PACKED = 9


def dot(a, b, dims):
    return lax.dot_general(a, b, (dims, ((), ())), precision=HIGHEST, preferred_element_type=F32)


def sub_row(tile, row):
    return jnp.broadcast_to(tile[row:row + 1, :], (8, NB))


def lane_col(tile, lane):
    return jnp.broadcast_to(tile[:, lane:lane + 1], (8, NB))


def factor_inverse(tiles_of, inv_ref):
    sub = lax.broadcasted_iota(jnp.int32, (8, NB), 0)
    lane = lax.broadcasted_iota(jnp.int32, (8, NB), 1)
    tiles = [list(t) for t in tiles_of]
    for k in range(BLOCKS):
        inside = (lane >= 8 * k) & (lane < 8 * k + 8)
        for e in range(len(tiles)):
            T = tiles[e]
            C = [lane_col(T[k], 8 * k + m) for m in range(8)]
            J = jnp.where(inside, jnp.where(lane - 8 * k == sub, 1.0, 0.0).astype(F32), T[k])
            forward = J
            rdiag = jnp.zeros((8, NB), F32)
            for j in range(8):
                r = 1.0 / sub_row(C[j], j)
                mult = jnp.where(sub == j, 0.0, C[j] * r)
                row = sub_row(J, j)
                forward = jnp.where(sub == j, J, forward)
                rdiag = jnp.where(sub == j, r, rdiag)
                for m in range(j + 1, 8):
                    C[m] = C[m] - mult * sub_row(C[m], j)
                J = J - mult * row
            J = J * rdiag
            inv_ref[e, 8 * k:8 * k + 8, :] = jnp.where(lane <= sub + 8 * k, forward * jnp.sqrt(rdiag), 0.0)
            if k + 1 < BLOCKS:
                rows = [sub_row(J, m) for m in range(8)]
                for t in range(k + 1, BLOCKS):
                    old = T[t]
                    new = jnp.where(inside, 0.0, old)
                    for m in range(8):
                        new = new - lane_col(old, 8 * k + m) * rows[m]
                    T[t] = new


def pack_lower(inv, packed, e):
    lane = lax.broadcasted_iota(jnp.int32, (8, NB), 1)
    for k in range(7):
        other = pltpu.roll(inv[e, 8 * (14 - k):8 * (15 - k), :], 8 * k + 8, 1)
        packed[e, k] = jnp.where(lane < 8 * k + 8, inv[e, 8 * k:8 * k + 8, :], other)
    packed[e, 7] = inv[e, 56:64, :]
    packed[e, 8] = inv[e, 120:128, :]


def unpack_lower(packed, s, e):
    lane = lax.broadcasted_iota(jnp.int32, (8, NB), 1)
    tiles = [None] * BLOCKS
    for k in range(7):
        tile = packed[s, e, k]
        tiles[k] = jnp.where(lane < 8 * k + 8, tile, 0.0)
        tiles[14 - k] = jnp.where(lane < 120 - 8 * k, pltpu.roll(tile, 120 - 8 * k, 1), 0.0)
    tiles[7] = packed[s, e, 7]
    tiles[15] = packed[s, e, 8]
    return jnp.concatenate(tiles, axis=0)


def main_kernel(pot_hbm, basis_ref, first_out, second_out,
                pot_ref, basis, low_x, high_x, low_z, high_z, corner,
                scaled, fa, fb, inner, stencil, gram, inv, face_z, got_face, packed, got_packed,
                crossed, first, second,
                basis_sem, halo_send, halo_recv, face_send, face_recv, pack_send, pack_recv,
                send_sem, recv_sem, own_sem):
    ex, ez = lax.axis_index("ex"), lax.axis_index("ez")
    nx, nz = lax.axis_size("ex"), lax.axis_size("ez")
    xs = {-1: lax.rem(ex + nx - 1, nx), 0: ex, 1: lax.rem(ex + 1, nx)}
    zs = {-1: lax.rem(ez + nz - 1, nz), 0: ez, 1: lax.rem(ez + 1, nz)}
    peers = [lax.rem(ez + k, nz) for k in range(1, nz)]
    loads = [pltpu.make_async_copy(basis_ref.at[e], basis.at[e], basis_sem.at[e]) for e in range(EY)]
    loads.append(pltpu.make_async_copy(pot_hbm, pot_ref, basis_sem.at[EY]))
    for load in loads:
        load.start()
    barrier = pltpu.get_barrier_semaphore()
    partners = [(ex, p) for p in peers] + [(xs[dx], zs[dz]) for dx, dz in SIDES if dx != 0]
    for target in partners:
        pl.semaphore_signal(barrier, inc=1, device_id=target, device_id_type=MESH)
    pl.semaphore_wait(barrier, len(partners))

    def send(source, landing, send_at, recv_at, target):
        copy = pltpu.make_async_remote_copy(
            src_ref=source, dst_ref=landing, send_sem=send_at, recv_sem=recv_at,
            device_id=target, device_id_type=MESH)
        copy.start()
        return copy

    landings = [low_x, high_x, low_z, high_z] + [corner.at[c] for c in range(4)]
    halo = []
    for n, (dx, dz) in enumerate(SIDES):
        part = pot_hbm if dx == 0 else pot_hbm.at[pl.ds(G - 2 if dx == 1 else 0, 2)]
        halo.append(send(part, landings[n], halo_send.at[n], halo_recv.at[n], (xs[dx], zs[dz])))

    sub = lax.broadcasted_iota(jnp.int32, (8, NB), 0)
    zero_slab = jnp.zeros((SLAB, NB), F32)
    for buf in (fa, fb):
        for e in range(EY):
            buf[e, 0:SLAB, :] = zero_slab
            buf[e, SLAB + ROWS:2 * SLAB + ROWS, :] = zero_slab
    for load in loads:
        load.wait()

    @pl.loop(0, BOX)
    def _(x):
        for e in range(EY):
            base = pl.multiple_of(x * SLAB, 16)
            fa[e, pl.ds(pl.multiple_of(base + SLAB, 8), SLAB), :] = basis[e, pl.ds(base, SLAB), :].astype(F32)

    for copy in halo:
        copy.wait_recv()

    def spread(x, low, mid, high):
        lower = (jnp.concatenate([low[6:8], mid[0:6]], axis=0) - 3.5) * (1.0 / 5.5)
        upper = (jnp.concatenate([mid[6:8], high[0:6]], axis=0) - 3.5) * (1.0 / 5.5)
        for y in range(16):
            a = jnp.broadcast_to(lower[:, y:y + 1], (8, NB))
            b = jnp.broadcast_to(upper[:, y:y + 1], (8, NB))
            for e in range(EY):
                at = (y - 8 * e + 2) % 16
                if at < BOX:
                    base = x * SLAB + at * BOX
                    scaled[e, pl.ds(base, 8), :] = a
                    scaled[e, pl.ds(base + 8, 4), :] = b[0:4, :]

    @pl.loop(0, 2)
    def _(x):
        spread(x, corner[0, x], low_x[x], corner[1, x])
        spread(x + 2 + G, corner[2, x], high_x[x], corner[3, x])

    @pl.loop(0, G)
    def _(x):
        spread(x + 2, low_z[x], pot_ref[x], high_z[x])

    def sweep(src, dst, older):
        @pl.loop(0, BOX)
        def _(x):
            for e in range(EY):
                for t in range(SLAB // 8):
                    at = pl.multiple_of(x * SLAB + 8 * t, 8)
                    o = SLAB + at
                    center = src[e, pl.ds(o, 8), :]
                    beside = src[e, pl.ds(o - SLAB, 8), :] + src[e, pl.ds(o + SLAB, 8), :]
                    if t > 0:
                        v = src[e, pl.ds(o - BOX, 8), :]
                        beside = beside + (jnp.where(sub < 4, 0.0, v) if t == 1 else v)
                    if t < SLAB // 8 - 1:
                        v = src[e, pl.ds(o + BOX, 8), :]
                        beside = beside + (jnp.where(sub >= 4, 0.0, v) if t == SLAB // 8 - 2 else v)
                    v = src[e, pl.ds(o - 1, 8), :]
                    beside = beside + (v if t % 3 == 2 else jnp.where(sub == (0, 4)[t % 3], 0.0, v))
                    v = src[e, pl.ds(o + 1, 8), :]
                    beside = beside + (v if t % 3 == 0 else jnp.where(sub == (0, 3, 7)[t % 3], 0.0, v))
                    a = scaled[e, pl.ds(at, 8), :]
                    if older is None:
                        new = a * center - (0.5 / 5.5) * beside
                    else:
                        new = 2.0 * (a * center) - (1.0 / 5.5) * beside - older[e, pl.ds(o, 8), :]
                    dst[e, pl.ds(o, 8), :] = new

    sweep(fa, fb, None)
    sweep(fb, fa, fa)
    sweep(fa, fb, fb)

    def corner_row(x, y):
        return (x + 2) * SLAB + (y + 2) * BOX + 2

    for e in range(EY):
        for x in range(G):
            for y in range(G):
                p = SLAB + corner_row(x, y)
                inner[e, 64 * x + 8 * y:64 * x + 8 * y + 8, :] = fb[e, p:p + 8, :]
        face_z[e, 0:64, :] = inner[e, pl.ds(0, 64, stride=8), :]
        face_z[e, 64:128, :] = inner[e, pl.ds(1, 64, stride=8), :]
    faces = []
    for e in range(EY):
        faces.append(send(inner.at[e, pl.ds(0, 128)], got_face.at[0, e], face_send.at[0, e], face_recv.at[0, e], (xs[-1], ez)))
        faces.append(send(face_z.at[e], got_face.at[1, e], face_send.at[1, e], face_recv.at[1, e], (ex, zs[-1])))

    for e in range(EY):
        full = fb[e, SLAB:SLAB + ROWS, :]
        high = full.astype(BF16)
        rest = (full - high.astype(F32)).astype(BF16)
        both = jnp.concatenate([high, rest], axis=1)
        prod = lax.dot_general(both, both, (((0,), (0,)), ((), ())), preferred_element_type=F32)
        cross = prod[0:NB, NB:2 * NB]
        gram[e] = prod[0:NB, 0:NB] + (cross + cross.T) + prod[NB:2 * NB, NB:2 * NB]

    up = jnp.where(sub == 0, 0.0, jnp.where((sub == 1) | (sub == 7), 0.25, 0.5))
    down = jnp.where(sub == 7, 0.0, jnp.where((sub == 0) | (sub == 6), 0.25, 0.5))

    def edge(i):
        return 0.25 if i in (0, 6) else 0.5

    def tile(e, x, y):
        return inner[e, 64 * x + 8 * y:64 * x + 8 * y + 8, :]

    def layer(e, d, i):
        if d == 0:
            return inner[e, 64 * i:64 * i + 64, :]
        if d == 1:
            return jnp.concatenate([tile(e, x, i) for x in range(G)], axis=0)
        return inner[e, pl.ds(i, 64, stride=8), :]

    def plus_side(e, d):
        last = layer(e, d, 7)
        return jnp.concatenate([-0.5 * last - 0.25 * layer(e, d, 6), -0.25 * last], axis=0)

    for e in range(EY):
        for x in range(G):
            for y in range(G):
                p = corner_row(x, y)
                c = tile(e, x, y)
                out = (5.5 * scaled[e, p:p + 8, :] + 6.5) * c
                if x > 0:
                    out = out - edge(x - 1) * tile(e, x - 1, y)
                if x < G - 1:
                    out = out - edge(x) * tile(e, x + 1, y)
                if y > 0:
                    out = out - edge(y - 1) * tile(e, x, y - 1)
                if y < G - 1:
                    out = out - edge(y) * tile(e, x, y + 1)
                out = out - up * pltpu.roll(c, 1, 0) - down * pltpu.roll(c, 7, 0)
                stencil[e, 64 * x + 8 * y:64 * x + 8 * y + 8, :] = out
        crossed[e, :, 0:NB] = dot(inner[e], stencil[e], ((0,), (0,)))
        minus_y = jnp.concatenate([layer(1 - e, 1, 0), layer(1 - e, 1, 1)], axis=0)
        crossed[e, :, NB:2 * NB] = dot(plus_side(e, 1), minus_y, ((0,), (0,)))

    factor_inverse([[gram[e, 8 * t:8 * t + 8, :] for t in range(BLOCKS)] for e in range(EY)], inv)

    packs = []
    for e in range(EY):
        pack_lower(inv, packed, e)
    for s, target in enumerate([(xs[-1], ez), (ex, zs[-1])]):
        packs.append(send(packed, got_packed.at[s], pack_send.at[s], pack_recv.at[s], target))

    def spread_rows(half, source, landing):
        copies = [send(source.at[p], landing.at[ez], send_sem.at[half, k], recv_sem.at[half, k], (ex, p))
                  for k, p in enumerate(peers)]
        own = pltpu.make_async_copy(source.at[ez], landing.at[ez], own_sem.at[half])
        own.start()
        return copies, own

    for e in range(EY):
        mixed = dot(inv[e], crossed[e, :, 0:2 * NB], ((1,), (0,)))
        diag = dot(mixed[:, 0:NB], inv[e], ((1,), (1,)))
        side = dot(mixed[:, NB:2 * NB], inv[1 - e], ((1,), (1,)))
        for r in range(BLOCKS):
            first[r, e] = diag[8 * r:8 * r + 8, :]
            first[r, EY + e] = side[8 * r:8 * r + 8, :]
    first_copies, first_own = spread_rows(0, first, first_out)

    for copy in faces:
        copy.wait_recv()
    for e in range(EY):
        raw = jnp.concatenate([dot(plus_side(e, 2 * s), got_face[s, e], ((0,), (0,))) for s in range(2)], axis=1)
        crossed[e, :, 0:2 * NB] = dot(inv[e], raw, ((1,), (0,)))
    for s in (1, 0):
        packs[s].wait_recv()
        for e in range(EY):
            block = dot(crossed[e, :, NB * s:NB * s + NB], unpack_lower(got_packed, s, e), ((1,), (1,)))
            for r in range(BLOCKS):
                second[r, s * EY + e] = block[8 * r:8 * r + 8, :]
    second_copies, second_own = spread_rows(1, second, second_out)

    for copy in first_copies + second_copies:
        copy.wait_recv()
    first_own.wait()
    second_own.wait()
    for copy in halo + faces + packs + first_copies + second_copies:
        copy.wait_send()


def main_call(block, starts):
    anywhere = pl.BlockSpec(memory_space=pl.ANY)
    hbm = pl.BlockSpec(memory_space=pltpu.HBM)
    part = (G, 2 * G)
    rows = (BLOCKS, 2 * EY, 8, NB)
    dma = pltpu.SemaphoreType.DMA
    return pl.pallas_call(
        main_kernel,
        out_shape=(jax.ShapeDtypeStruct(rows, F32), jax.ShapeDtypeStruct(rows, F32)),
        in_specs=[hbm, hbm],
        out_specs=(anywhere, anywhere),
        scratch_shapes=[
            pltpu.VMEM((G,) + part, F32),
            pltpu.VMEM((EY, ROWS, NB), BF16),
            pltpu.VMEM((2,) + part, F32),
            pltpu.VMEM((2,) + part, F32),
            pltpu.VMEM((G,) + part, F32),
            pltpu.VMEM((G,) + part, F32),
            pltpu.VMEM((4, 2) + part, F32),
            pltpu.VMEM((EY, ROWS, NB), F32),
            pltpu.VMEM((EY, ROWS + 2 * SLAB, NB), F32),
            pltpu.VMEM((EY, ROWS + 2 * SLAB, NB), F32),
            pltpu.VMEM((EY, G ** 3, NB), F32),
            pltpu.VMEM((EY, G ** 3, NB), F32),
            pltpu.VMEM((EY, NB, NB), F32),
            pltpu.VMEM((EY, NB, NB), F32),
            pltpu.VMEM((EY, NB, NB), F32),
            pltpu.VMEM((2, EY, NB, NB), F32),
            pltpu.VMEM((EY, PACKED, 8, NB), F32),
            pltpu.VMEM((2, EY, PACKED, 8, NB), F32),
            pltpu.VMEM((EY, NB, 2 * NB), F32),
            pltpu.VMEM(rows, F32),
            pltpu.VMEM(rows, F32),
            dma((EY + 1,)), dma((8,)), dma((8,)), dma((2, EY)), dma((2, EY)), dma((2,)), dma((2,)),
            dma((2, BLOCKS - 1)), dma((2, BLOCKS - 1)), dma((2,)),
        ],
        compiler_params=pltpu.CompilerParams(
            collective_id=0, has_side_effects=True, vmem_limit_bytes=40 * 2**20),
    )(block, starts)


def place_kernel(first_ref, second_ref, diag_ref, coup_ref):
    @pl.loop(0, BLOCKS)
    def _(z):
        for e in range(EY):
            diag_ref[pl.ds(z * EY + e, 8, stride=BLOCKS * EY), :] = first_ref[z, e]
            for k in range(3):
                tile = first_ref[z, EY + e] if k == 1 else second_ref[z, (k // 2) * EY + e]
                coup_ref[pl.ds(z * 3 * EY + k * EY + e, 8, stride=BLOCKS * 3 * EY), :] = tile


def place_call(first, second):
    vm = pl.BlockSpec(memory_space=pltpu.VMEM)
    return pl.pallas_call(
        place_kernel,
        out_shape=(
            jax.ShapeDtypeStruct((8 * BLOCKS * EY, NB), F32),
            jax.ShapeDtypeStruct((8 * BLOCKS * 3 * EY, NB), F32),
        ),
        in_specs=[vm, vm],
        out_specs=(vm, vm),
        compiler_params=pltpu.CompilerParams(vmem_limit_bytes=4 * 2**20),
    )(first, second)


def local(potential, basis_start):
    block = jnp.transpose(potential, (0, 2, 1))
    block = pltpu.with_memory_space_constraint(block, pltpu.HBM)
    starts = pltpu.with_memory_space_constraint(basis_start.reshape(EY, ROWS, NB), pltpu.HBM)
    first, second = main_call(block, starts)
    diag, coup = place_call(first, second)
    coup = coup.reshape(8, BLOCKS, 3, EY, NB).transpose(0, 1, 3, 2, 4)
    return diag.reshape(1, 8, BLOCKS, EY, NB), coup[None]


def solution(mesh):
    return jax.shard_map(
        local,
        mesh=mesh,
        in_specs=(P("ex", None, "ez"), P("ex", "ez", None, None, None)),
        out_specs=(P("ex", "ez", None, None, None), P("ex", "ez", None, None, None, None)),
        check_vma=False,
    )
```

```python
import jax
import jax.numpy as jnp
from jax import lax
from jax.experimental import pallas as pl
from jax.experimental.pallas import tpu as pltpu
from jax.sharding import PartitionSpec as P

G, BOX, NB, EY = 8, 12, 128, 2
ROWS = BOX ** 3
SLAB = BOX * BOX
BLOCKS = NB // 8
HIGHEST = lax.Precision.HIGHEST
F32 = jnp.float32
BF16 = jnp.bfloat16
MESH = pl.DeviceIdType.MESH
SIDES = ((1, 0), (-1, 0), (0, 1), (0, -1), (1, 1), (1, -1), (-1, 1), (-1, -1))
PANEL = 4


def dot(a, b, dims):
    return lax.dot_general(a, b, (dims, ((), ())), precision=HIGHEST, preferred_element_type=F32)


def sub_row(tile, row):
    return jnp.broadcast_to(tile[row:row + 1, :], (8, NB))


def lane_col(tile, lane):
    return jnp.broadcast_to(tile[:, lane:lane + 1], (8, NB))


def halves(a):
    high = a.astype(BF16)
    return high, (a - high.astype(F32)).astype(BF16)


def dot3(a, b, dims):
    (a_high, a_low), (b_high, b_low) = halves(a), halves(b)

    def product(x, y):
        return lax.dot_general(x, y, (dims, ((), ())), preferred_element_type=F32)
    wide = product(jnp.concatenate([a_high, a_low], axis=dims[0][0]), jnp.concatenate([b_high, b_high], axis=dims[1][0]))
    return wide + product(a_high, b_low)


def factor_inverse(tiles_of, inv_ref, after_panel):
    sub = lax.broadcasted_iota(jnp.int32, (8, NB), 0)
    lane = lax.broadcasted_iota(jnp.int32, (8, NB), 1)
    zero = jnp.zeros((8, NB), F32)
    tiles = [list(t) for t in tiles_of]
    for p in range(BLOCKS // PANEL):
        first = PANEL * (p + 1)
        full = [[None] * PANEL for _ in tiles]
        for q in range(PANEL):
            k = PANEL * p + q
            inside = (lane >= 8 * k) & (lane < 8 * k + 8)
            for e, T in enumerate(tiles):
                C = [lane_col(T[k], 8 * k + m) for m in range(8)]
                J = jnp.where(inside, jnp.where(lane - 8 * k == sub, 1.0, 0.0).astype(F32), T[k])
                forward, rdiag = J, zero
                for j in range(8):
                    r = 1.0 / sub_row(C[j], j)
                    mult = jnp.where(sub == j, 0.0, C[j] * r)
                    row = sub_row(J, j)
                    forward = jnp.where(sub == j, J, forward)
                    rdiag = jnp.where(sub == j, r, rdiag)
                    for m in range(j + 1, 8):
                        C[m] = C[m] - mult * sub_row(C[m], j)
                    J = J - mult * row
                J = J * rdiag
                inv_ref[e, 8 * k:8 * k + 8, :] = jnp.where(lane <= sub + 8 * k, forward * jnp.sqrt(rdiag), 0.0)
                rows = [sub_row(J, m) for m in range(8)]

                def update(old):
                    new = jnp.where(inside, 0.0, old)
                    for m in range(8):
                        new = new - lane_col(old, 8 * k + m) * rows[m]
                    return new
                for q2 in range(q + 1, PANEL):
                    T[PANEL * p + q2] = update(T[PANEL * p + q2])
                if first < BLOCKS:
                    full[e][:q] = [update(old) for old in full[e][:q]]
                    full[e][q] = J
        after_panel(p)
        if first < BLOCKS:
            inside = (lane >= 8 * PANEL * p) & (lane < 8 * first)
            for e, T in enumerate(tiles):
                pivot = jnp.concatenate([zero] * (PANEL * p) + full[e] + [zero] * (BLOCKS - first), axis=0)
                change = dot(jnp.concatenate(T[first:], axis=0), pivot, ((1,), (0,)))
                for t in range(first, BLOCKS):
                    T[t] = jnp.where(inside, 0.0, T[t]) - change[8 * (t - first):8 * (t - first) + 8, :]


def main_kernel(pot_hbm, basis_ref, first_out, second_out, third_out,
                pot_ref, basis, low_x, high_x, low_z, high_z, corner,
                scaled, fa, fb, inner, stencil, gram, inv, minus, plus, turned, got_turned,
                crossed, first, second, third,
                basis_sem, halo_send, halo_recv, turn_send, turn_recv,
                send_sem, recv_sem, own_sem):
    ex, ez = lax.axis_index("ex"), lax.axis_index("ez")
    nx, nz = lax.axis_size("ex"), lax.axis_size("ez")
    xs = {-1: lax.rem(ex + nx - 1, nx), 0: ex, 1: lax.rem(ex + 1, nx)}
    zs = {-1: lax.rem(ez + nz - 1, nz), 0: ez, 1: lax.rem(ez + 1, nz)}
    peers = [lax.rem(ez + k, nz) for k in range(1, nz)]
    loads = [pltpu.make_async_copy(basis_ref.at[e], basis.at[e], basis_sem.at[e]) for e in range(EY)]
    loads.append(pltpu.make_async_copy(pot_hbm, pot_ref, basis_sem.at[EY]))
    for load in loads:
        load.start()
    barrier = pltpu.get_barrier_semaphore()
    partners = [(ex, p) for p in peers] + [(xs[dx], zs[dz]) for dx, dz in SIDES if dx != 0]
    for target in partners:
        pl.semaphore_signal(barrier, inc=1, device_id=target, device_id_type=MESH)
    pl.semaphore_wait(barrier, len(partners))

    def send(source, landing, send_at, recv_at, target):
        copy = pltpu.make_async_remote_copy(
            src_ref=source, dst_ref=landing, send_sem=send_at, recv_sem=recv_at,
            device_id=target, device_id_type=MESH)
        copy.start()
        return copy

    landings = [low_x, high_x, low_z, high_z] + [corner.at[c] for c in range(4)]
    halo = []
    for n, (dx, dz) in enumerate(SIDES):
        part = pot_hbm if dx == 0 else pot_hbm.at[pl.ds(G - 2 if dx == 1 else 0, 2)]
        halo.append(send(part, landings[n], halo_send.at[n], halo_recv.at[n], (xs[dx], zs[dz])))

    sub = lax.broadcasted_iota(jnp.int32, (8, NB), 0)
    zero_slab = jnp.zeros((SLAB, NB), F32)
    for buf in (fa, fb):
        for e in range(EY):
            buf[e, 0:SLAB, :] = zero_slab
            buf[e, SLAB + ROWS:2 * SLAB + ROWS, :] = zero_slab
    for load in loads:
        load.wait()

    @pl.loop(0, BOX)
    def _(x):
        for e in range(EY):
            base = pl.multiple_of(x * SLAB, 16)
            fa[e, pl.ds(pl.multiple_of(base + SLAB, 8), SLAB), :] = basis[e, pl.ds(base, SLAB), :].astype(F32)

    for copy in halo:
        copy.wait_recv()

    def spread(x, low, mid, high):
        lower = (jnp.concatenate([low[6:8], mid[0:6]], axis=0) - 3.5) * (1.0 / 5.5)
        upper = (jnp.concatenate([mid[6:8], high[0:6]], axis=0) - 3.5) * (1.0 / 5.5)
        for y in range(16):
            a = jnp.broadcast_to(lower[:, y:y + 1], (8, NB))
            b = jnp.broadcast_to(upper[:, y:y + 1], (8, NB))
            for e in range(EY):
                at = (y - 8 * e + 2) % 16
                if at < BOX:
                    base = x * SLAB + at * BOX
                    scaled[e, pl.ds(base, 8), :] = a
                    scaled[e, pl.ds(base + 8, 4), :] = b[0:4, :]

    @pl.loop(0, 2)
    def _(x):
        spread(x, corner[0, x], low_x[x], corner[1, x])
        spread(x + 2 + G, corner[2, x], high_x[x], corner[3, x])

    @pl.loop(0, G)
    def _(x):
        spread(x + 2, low_z[x], pot_ref[x], high_z[x])

    def sweep(src, dst, older):
        @pl.loop(0, BOX)
        def _(x):
            for e in range(EY):
                for t in range(SLAB // 8):
                    at = pl.multiple_of(x * SLAB + 8 * t, 8)
                    o = SLAB + at
                    center = src[e, pl.ds(o, 8), :]
                    beside = src[e, pl.ds(o - SLAB, 8), :] + src[e, pl.ds(o + SLAB, 8), :]
                    if t > 0:
                        v = src[e, pl.ds(o - BOX, 8), :]
                        beside = beside + (jnp.where(sub < 4, 0.0, v) if t == 1 else v)
                    if t < SLAB // 8 - 1:
                        v = src[e, pl.ds(o + BOX, 8), :]
                        beside = beside + (jnp.where(sub >= 4, 0.0, v) if t == SLAB // 8 - 2 else v)
                    v = src[e, pl.ds(o - 1, 8), :]
                    beside = beside + (v if t % 3 == 2 else jnp.where(sub == (0, 4)[t % 3], 0.0, v))
                    v = src[e, pl.ds(o + 1, 8), :]
                    beside = beside + (v if t % 3 == 0 else jnp.where(sub == (0, 3, 7)[t % 3], 0.0, v))
                    a = scaled[e, pl.ds(at, 8), :]
                    if older is None:
                        new = a * center - (0.5 / 5.5) * beside
                    else:
                        new = 2.0 * (a * center) - (1.0 / 5.5) * beside - older[e, pl.ds(o, 8), :]
                    dst[e, pl.ds(o, 8), :] = new

    sweep(fa, fb, None)
    sweep(fb, fa, fa)
    sweep(fa, fb, fb)

    def corner_row(x, y):
        return (x + 2) * SLAB + (y + 2) * BOX + 2

    for e in range(EY):
        for x in range(G):
            for y in range(G):
                p = SLAB + corner_row(x, y)
                inner[e, 64 * x + 8 * y:64 * x + 8 * y + 8, :] = fb[e, p:p + 8, :]

    for e in range(EY):
        full = fb[e, SLAB:SLAB + ROWS, :]
        high = full.astype(BF16)
        rest = (full - high.astype(F32)).astype(BF16)
        both = jnp.concatenate([high, rest], axis=1)
        prod = lax.dot_general(both, both, (((0,), (0,)), ((), ())), preferred_element_type=F32)
        cross = prod[0:NB, NB:2 * NB]
        gram[e] = prod[0:NB, 0:NB] + (cross + cross.T) + prod[NB:2 * NB, NB:2 * NB]

    up = jnp.where(sub == 0, 0.0, jnp.where((sub == 1) | (sub == 7), 0.25, 0.5))
    down = jnp.where(sub == 7, 0.0, jnp.where((sub == 0) | (sub == 6), 0.25, 0.5))

    def edge(i):
        return 0.25 if i in (0, 6) else 0.5

    def tile(e, x, y):
        return inner[e, 64 * x + 8 * y:64 * x + 8 * y + 8, :]

    def layer(e, d, i):
        if d == 0:
            return inner[e, 64 * i:64 * i + 64, :]
        if d == 1:
            return jnp.concatenate([tile(e, x, i) for x in range(G)], axis=0)
        return inner[e, pl.ds(i, 64, stride=8), :]

    def plus_side(e, d):
        last = layer(e, d, 7)
        return jnp.concatenate([-0.5 * last - 0.25 * layer(e, d, 6), -0.25 * last], axis=0)

    for e in range(EY):
        for x in range(G):
            for y in range(G):
                p = corner_row(x, y)
                c = tile(e, x, y)
                out = (5.5 * scaled[e, p:p + 8, :] + 6.5) * c
                if x > 0:
                    out = out - edge(x - 1) * tile(e, x - 1, y)
                if x < G - 1:
                    out = out - edge(x) * tile(e, x + 1, y)
                if y > 0:
                    out = out - edge(y - 1) * tile(e, x, y - 1)
                if y < G - 1:
                    out = out - edge(y) * tile(e, x, y + 1)
                out = out - up * pltpu.roll(c, 1, 0) - down * pltpu.roll(c, 7, 0)
                stencil[e, 64 * x + 8 * y:64 * x + 8 * y + 8, :] = out
        crossed[e, :, 0:NB] = dot(inner[e], stencil[e], ((0,), (0,)))
        minus_y = jnp.concatenate([layer(1 - e, 1, 0), layer(1 - e, 1, 1)], axis=0)
        crossed[e, :, NB:2 * NB] = dot(plus_side(e, 1), minus_y, ((0,), (0,)))

    for e in range(EY):
        for s in range(2):
            minus[e, 128 * s:128 * s + 64, :] = layer(e, 2 * s, 0)
            minus[e, 128 * s + 64:128 * s + 128, :] = layer(e, 2 * s, 1)
            plus[e, 128 * s:128 * s + 128, :] = plus_side(e, 2 * s)
    turns = []

    def send_turned(p):
        rows = 8 * PANEL
        for e in range(EY):
            part = dot3(inv[e, rows * p:rows * p + rows, :], minus[e], ((1,), (1,)))
            for s in range(2):
                turned[s, p, e] = part[:, NB * s:NB * s + NB]
        for s, target in enumerate([(xs[-1], ez), (ex, zs[-1])]):
            turns.append(send(turned.at[s, p], got_turned.at[s, p], turn_send.at[s, p], turn_recv.at[s, p], target))

    factor_inverse([[gram[e, 8 * t:8 * t + 8, :] for t in range(BLOCKS)] for e in range(EY)], inv, send_turned)

    def spread_rows(part, source, landing):
        copies = [send(source.at[p], landing.at[ez], send_sem.at[part, k], recv_sem.at[part, k], (ex, p))
                  for k, p in enumerate(peers)]
        own = pltpu.make_async_copy(source.at[ez], landing.at[ez], own_sem.at[part])
        own.start()
        return copies, own

    for e in range(EY):
        mixed = dot3(inv[e], crossed[e, :, 0:2 * NB], ((1,), (0,)))
        diag = dot3(mixed[:, 0:NB], inv[e], ((1,), (1,)))
        side = dot3(mixed[:, NB:2 * NB], inv[1 - e], ((1,), (1,)))
        for r in range(BLOCKS):
            first[r, e] = diag[8 * r:8 * r + 8, :]
            first[r, EY + e] = side[8 * r:8 * r + 8, :]
    first_copies, first_own = spread_rows(0, first, first_out)

    for e in range(EY):
        crossed[e] = dot3(inv[e], plus[e], ((1,), (1,)))
    parts = [(first_copies, first_own)]
    for s, source, landing in ((1, third, third_out), (0, second, second_out)):
        for copy in turns[s::2]:
            copy.wait_recv()
        for e in range(EY):
            other = jnp.concatenate([got_turned[s, p, e] for p in range(BLOCKS // PANEL)], axis=0)
            block = dot3(crossed[e, :, NB * s:NB * s + NB], other, ((1,), (1,)))
            for r in range(BLOCKS):
                source[r, e] = block[8 * r:8 * r + 8, :]
        parts.append(spread_rows(1 + s, source, landing))

    for copies, own in parts:
        for copy in copies:
            copy.wait_recv()
        own.wait()
    for copy in halo + turns + [copy for copies, _ in parts for copy in copies]:
        copy.wait_send()


def main_call(block, starts):
    anywhere = pl.BlockSpec(memory_space=pl.ANY)
    hbm = pl.BlockSpec(memory_space=pltpu.HBM)
    part = (G, 2 * G)
    panels = (2, BLOCKS // PANEL, EY, 8 * PANEL, NB)
    rows, half = (BLOCKS, 2 * EY, 8, NB), (BLOCKS, EY, 8, NB)
    dma = pltpu.SemaphoreType.DMA
    return pl.pallas_call(
        main_kernel,
        out_shape=tuple(jax.ShapeDtypeStruct(r, F32) for r in (rows, half, half)),
        in_specs=[hbm, hbm],
        out_specs=(anywhere,) * 3,
        scratch_shapes=[
            pltpu.VMEM((G,) + part, F32),
            pltpu.VMEM((EY, ROWS, NB), BF16),
            pltpu.VMEM((2,) + part, F32),
            pltpu.VMEM((2,) + part, F32),
            pltpu.VMEM((G,) + part, F32),
            pltpu.VMEM((G,) + part, F32),
            pltpu.VMEM((4, 2) + part, F32),
            pltpu.VMEM((EY, ROWS, NB), F32),
            pltpu.VMEM((EY, ROWS + 2 * SLAB, NB), F32),
            pltpu.VMEM((EY, ROWS + 2 * SLAB, NB), F32),
            pltpu.VMEM((EY, G ** 3, NB), F32),
            pltpu.VMEM((EY, G ** 3, NB), F32),
            pltpu.VMEM((EY, NB, NB), F32),
            pltpu.VMEM((EY, NB, NB), F32),
            pltpu.VMEM((EY, 2 * NB, NB), F32),
            pltpu.VMEM((EY, 2 * NB, NB), F32),
            pltpu.VMEM(panels, F32),
            pltpu.VMEM(panels, F32),
            pltpu.VMEM((EY, NB, 2 * NB), F32),
            pltpu.VMEM(rows, F32),
            pltpu.VMEM(half, F32),
            pltpu.VMEM(half, F32),
            dma((EY + 1,)), dma((8,)), dma((8,)), dma((2, BLOCKS // PANEL)), dma((2, BLOCKS // PANEL)),
            dma((3, BLOCKS - 1)), dma((3, BLOCKS - 1)), dma((3,)),
        ],
        compiler_params=pltpu.CompilerParams(
            collective_id=0, has_side_effects=True, vmem_limit_bytes=40 * 2**20),
    )(block, starts)


def place_kernel(first_ref, second_ref, third_ref, diag_ref, coup_ref):
    @pl.loop(0, BLOCKS)
    def _(z):
        for e in range(EY):
            diag_ref[pl.ds(z * EY + e, 8, stride=BLOCKS * EY), :] = first_ref[z, e]
            for k in range(3):
                tile = (second_ref[z, e], first_ref[z, EY + e], third_ref[z, e])[k]
                coup_ref[pl.ds(z * 3 * EY + k * EY + e, 8, stride=BLOCKS * 3 * EY), :] = tile


def place_call(*parts):
    vm = pl.BlockSpec(memory_space=pltpu.VMEM)
    return pl.pallas_call(
        place_kernel,
        out_shape=(
            jax.ShapeDtypeStruct((8 * BLOCKS * EY, NB), F32),
            jax.ShapeDtypeStruct((8 * BLOCKS * 3 * EY, NB), F32),
        ),
        in_specs=[vm] * 3,
        out_specs=(vm, vm),
        compiler_params=pltpu.CompilerParams(vmem_limit_bytes=4 * 2**20),
    )(*parts)


def local(potential, basis_start):
    block = jnp.transpose(potential, (0, 2, 1))
    block = pltpu.with_memory_space_constraint(block, pltpu.HBM)
    starts = pltpu.with_memory_space_constraint(basis_start.reshape(EY, ROWS, NB), pltpu.HBM)
    diag, coup = place_call(*main_call(block, starts))
    coup = coup.reshape(8, BLOCKS, 3, EY, NB).transpose(0, 1, 3, 2, 4)
    return diag.reshape(1, 8, BLOCKS, EY, NB), coup[None]


def solution(mesh):
    return jax.shard_map(
        local,
        mesh=mesh,
        in_specs=(P("ex", None, "ez"), P("ex", "ez", None, None, None)),
        out_specs=(P("ex", "ez", None, None, None), P("ex", "ez", None, None, None, None)),
        check_vma=False,
    )
```
